128 devices in a mesh: space: 8 (over x, core), win: 16 (over z, y).
Axes of the slice: x: 4, y: 4, z: 4, core: 2. Of those that a mesh axis runs over, the one named last changes fastest.
Arguments:
- snapshots: bfloat16 [128, 24576, 256], P('win', 'space'), as said below
- modes: bfloat16 [128, 24576, 256], P('win', 'space'), may hold values from -0.5 to 0.5
- amp_re: float32 [128, 128], P('win'), may hold values from -5 to 5
- amp_im: float32 [128, 128], P('win'), may hold values from -5 to 5
- growth: float32 [128, 128], P('win'), may hold values from -0.01171875 to 0.001953125
- freq: float32 [128, 128], P('win'), may hold values from -3.140625 to 3.140625
- mode_count: int32 [128], P('win'), may hold values from 8 to 128
- slot_window: int32 [128], P('win'), may hold values from 0 to 127, as said below
Outputs:
- gram: float32 [128, 256, 256], P('win')
The draws below stay inside these ranges and needn't reach their ends.
Inputs may be any that keep to these rules, and one draw needn't show every extreme that they name: slot_window is a permutation of the 128 windows; slot j holds a window of the same position in its block, slot_window[j] % 8 == j % 8; the 8 slots of one block hold windows of 8 different blocks. Each point's snapshots share one scale.
All inputs are finite; a program needn't handle non-finite values.
Results may differ from the reference program's by a relative error of at most 0.0026.
Values may be sent and summed in bfloat16 or wider, within the bound.
A program may use at most 192 MiB of HBM per device.

```python
import math
import jax
import jax.numpy as jnp
from jax import lax

K = 128
S = 256
WIN_DEV = 8
W = 128
POINTS = 24576


def draw_slot_window(key, part):
    nblocks = W // WIN_DEV
    key_perm, key_offset = jax.random.split(jax.random.fold_in(key, 11))
    order = jax.random.permutation(key_perm, nblocks)
    offsets = jax.random.permutation(key_offset, nblocks)[:WIN_DEV]
    dest = (order[:, None] + offsets[None, :]) % nblocks
    window = dest * WIN_DEV + jnp.arange(WIN_DEV)[None, :]
    return window.reshape(W).astype(jnp.int32)


def draw_snapshots(key, part):
    key_scale, key_base = jax.random.split(jax.random.fold_in(key, 23))
    scales = jnp.exp(jax.random.uniform(key_scale, (1, POINTS, 1), jnp.float32, math.log(0.25), math.log(2.5)))
    base = jnp.clip(jax.random.normal(key_base, (W, POINTS, S), jnp.float32), -6.0, 6.0)
    return (base * scales).astype(jnp.bfloat16)


def place_ends(array, stream_key, smallest, largest):
    longest = array.shape.index(max(array.shape))
    spots = []
    for shift in (0, 1):
        where = [jax.random.randint(jax.random.fold_in(stream_key, axis), (), 0, length) for axis, length in enumerate(array.shape)]
        where[longest] = (where[longest] + shift) % array.shape[longest]
        spots.append(tuple(where))
    return array.at[spots[0]].set(smallest).at[spots[1]].set(largest)


def block_levels(rng, dims, shards, least, top_value):
    factor_of = 1.0
    for dim, parts in shards:
        steps = jax.random.uniform(jax.random.fold_in(jax.random.fold_in(rng, 6), dim), (parts,), jnp.float32, least / len(shards), top_value / len(shards))
        factor_of = factor_of * jnp.repeat(jnp.exp(steps), dims[dim] // parts).reshape((-1,) + (1,) * (len(dims) - 1 - dim))
    return factor_of


def normal_values(rng, dims, spread, limit, shards=(), kind=jnp.bfloat16):
    values = spread * jax.random.normal(rng, dims, jnp.float32)
    if shards:
        values = values * block_levels(rng, dims, shards, -0.22, 0.18)
    return jnp.clip(values, -limit, limit).astype(kind)


def setup_inputs(seed: int = 0) -> dict:
    keys = jax.random.split(jax.random.key(seed), 9)
    snapshots = draw_snapshots(jax.random.fold_in(keys[8], 71), 0)
    modes = normal_values(keys[1], (W, POINTS, 2 * K), K ** -0.5, 0.5, ((0, 16), (1, 8)))
    amp_re = normal_values(keys[2], (W, K), 1.0, 5.0, ((0, 16),), jnp.float32)
    amp_im = normal_values(keys[3], (W, K), 1.0, 5.0, ((0, 16),), jnp.float32)
    growth = jnp.clip(-0.01171875 + 0.013671875 * jax.random.uniform(keys[4], (W, K), jnp.float32) ** block_levels(keys[4], (W, K), ((0, 16),), -0.2, 0.2), -0.01171875, 0.001953125)
    freq = jnp.clip(jax.random.uniform(keys[5], (W, K), jnp.float32, -3.140625, 3.140625), -3.140625, 3.140625)
    mode_count = place_ends(jax.random.randint(keys[6], (W,), 8, K + 1), jax.random.fold_in(keys[6], 1), 8, K).astype(jnp.int32)
    slot_window = draw_slot_window(jax.random.fold_in(keys[8], 71), 0)
    return dict(snapshots=snapshots, modes=modes, amp_re=amp_re, amp_im=amp_im, growth=growth, freq=freq, mode_count=mode_count, slot_window=slot_window)


def coefficients(amp_re, amp_im, growth, freq, mode_count):
    steps = jnp.arange(S).astype(jnp.float32)
    live = (jnp.arange(K, dtype=jnp.int32)[None, :] < mode_count[:, None]).astype(jnp.float32)
    decay = jnp.exp(growth[:, :, None] * steps) * live[:, :, None]
    angle = freq[:, :, None] * steps
    cosine = jnp.cos(angle)
    sine = jnp.sin(angle)
    real_part = (amp_re[:, :, None] * cosine - amp_im[:, :, None] * sine) * decay
    imag_part = (amp_re[:, :, None] * sine + amp_im[:, :, None] * cosine) * decay
    stacked = jnp.stack([real_part, -imag_part], axis=2)
    return stacked.reshape(amp_re.shape[0], 2 * K, S).astype(jnp.bfloat16)


def window_gram(slab, vectors, coef):
    recon = jnp.dot(vectors, coef, preferred_element_type=jnp.float32)
    resid = (slab.astype(jnp.float32) - recon).astype(jnp.bfloat16)
    return lax.dot_general(resid, resid, (((0,), (0,)), ((), ())), preferred_element_type=jnp.float32)


def reference(snapshots, modes, amp_re, amp_im, growth, freq, mode_count, slot_window):
    coef = coefficients(amp_re, amp_im, growth, freq, mode_count)
    slot_of = jnp.zeros((W,), jnp.int32).at[slot_window].set(jnp.arange(W, dtype=jnp.int32))

    def single(window):
        slot = slot_of[window]
        return window_gram(snapshots[window], modes[slot], coef[slot])

    grams = lax.map(single, jnp.arange(W, dtype=jnp.int32))
    return grams / POINTS
```

```python
import functools

import jax
import jax.numpy as jnp
from jax import lax
from jax.experimental import pallas as pl
from jax.experimental.pallas import tpu as pltpu
from jax.sharding import PartitionSpec as P

K = 128
S = 256
WIN_DEV = 8
NCH = 1
TP = 1536


def coefficients(amp_re, amp_im, growth, freq, mode_count):
    steps = jnp.arange(S).astype(jnp.float32)
    live = (jnp.arange(K, dtype=jnp.int32)[None, :] < mode_count[:, None]).astype(jnp.float32)
    decay = jnp.exp(growth[:, :, None] * steps) * live[:, :, None]
    angle = freq[:, :, None] * steps
    cosine = jnp.cos(angle)
    sine = jnp.sin(angle)
    real_part = (amp_re[:, :, None] * cosine - amp_im[:, :, None] * sine) * decay
    imag_part = (amp_re[:, :, None] * sine + amp_im[:, :, None] * cosine) * decay
    stacked = jnp.stack([real_part, -imag_part], axis=2)
    return stacked.reshape(amp_re.shape[0], 2 * K, S).astype(jnp.bfloat16)


def gram_kernel(src_ref, s_ref, m_ref, c_ref, o_ref):
    t = pl.program_id(1)

    @pl.when(t == 0)
    def _():
        o_ref[...] = jnp.zeros_like(o_ref)

    s = s_ref[0].astype(jnp.float32)
    recon = jnp.dot(m_ref[0], c_ref[0], preferred_element_type=jnp.float32)
    r = (s - recon).astype(jnp.bfloat16)
    half = S // 2
    dims = (((0,), (0,)), ((), ()))
    top = lax.dot_general(r[:, :half], r, dims, preferred_element_type=jnp.float32)
    low = lax.dot_general(r[:, half:], r[:, half:], dims, preferred_element_type=jnp.float32)
    o_ref[0, :, : 2 * half] += top
    o_ref[0, :, 2 * half :] += low


def chunk_gram(source, snapshots, got, coef, chunk):
    nw, _, s = snapshots.shape
    rows = got.shape[1]
    tp = min(TP, rows)
    nt = rows // tp
    base = chunk * nt
    return pl.pallas_call(
        gram_kernel,
        grid_spec=pltpu.PrefetchScalarGridSpec(
            num_scalar_prefetch=1,
            grid=(nw, nt),
            in_specs=[
                pl.BlockSpec((1, tp, s), lambda p, t, src: (p, base + t, 0)),
                pl.BlockSpec((1, tp, s), lambda p, t, src: (src[p], t, 0)),
                pl.BlockSpec((1, s, s), lambda p, t, src: (p, 0, 0)),
            ],
            out_specs=pl.BlockSpec((1, s // 2, 3 * s // 2), lambda p, t, src: (p, 0, 0)),
        ),
        out_shape=jax.ShapeDtypeStruct((nw, s // 2, 3 * s // 2), jnp.float32),
        compiler_params=pltpu.CompilerParams(
            dimension_semantics=("arbitrary", "arbitrary"),
            vmem_limit_bytes=48 * 1024 * 1024,
        ),
        cost_estimate=pl.CostEstimate(
            flops=int(nw * rows * s * s * 2 * 1.75),
            bytes_accessed=int(nw * rows * s * 2 * 2),
            transcendentals=0,
        ),
    )(source, snapshots, got, coef)


def on_device(snapshots, modes, amp_re, amp_im, growth, freq, mode_count, slot_window):
    nblocks = lax.axis_size("win")
    me = lax.axis_index("win")
    nw, rows, s = snapshots.shape
    points_all = rows * lax.axis_size("space")

    dest = slot_window // WIN_DEV
    hit = dest[None, :] == jnp.arange(nblocks, dtype=jnp.int32)[:, None]
    pick = jnp.sum(jnp.where(hit, jnp.arange(nw, dtype=jnp.int32)[None, :], 0), axis=1)

    cp = rows // NCH
    gots = []
    for k in range(NCH):
        part = modes[:, k * cp : (k + 1) * cp, :]
        sendbuf = jnp.take(part, pick, axis=0, mode="clip")
        gots.append(lax.all_to_all(sendbuf, "win", split_axis=0, concat_axis=0, tiled=True))

    extra = jnp.zeros((nw, K), jnp.float32)
    extra = extra.at[:, 0].set(mode_count.astype(jnp.float32))
    extra = extra.at[:, 1].set(slot_window.astype(jnp.float32))
    packed = jnp.concatenate([amp_re, amp_im, growth, freq, extra], axis=1)
    packed_all = lax.all_gather(packed, "win", axis=0, tiled=True)
    sw_all = packed_all[:, 4 * K + 1].astype(jnp.int32)
    wins = me * WIN_DEV + jnp.arange(nw, dtype=jnp.int32)
    slot_ids = jnp.arange(packed_all.shape[0], dtype=jnp.int32)
    slot = jnp.sum(jnp.where(sw_all[None, :] == wins[:, None], slot_ids[None, :], 0), axis=1)
    source = slot // WIN_DEV
    sel = jnp.take(packed_all, slot, axis=0, mode="clip")
    coef = coefficients(
        sel[:, 0:K],
        sel[:, K : 2 * K],
        sel[:, 2 * K : 3 * K],
        sel[:, 3 * K : 4 * K],
        sel[:, 4 * K].astype(jnp.int32),
    )

    part_sum = None
    for k in range(NCH):
        g = chunk_gram(source, snapshots, gots[k], coef, k)
        part_sum = g if part_sum is None else part_sum + g
    total = lax.psum(part_sum, "space") / points_all
    half = s // 2
    top = total[:, :, :s]
    mid = total[:, :, half:s]
    low = total[:, :, s:]
    bottom = jnp.concatenate([jnp.swapaxes(mid, 1, 2), low], axis=2)
    return jnp.concatenate([top, bottom], axis=1)


def solution(mesh):
    return jax.shard_map(
        on_device,
        mesh=mesh,
        in_specs=(
            P("win", "space", None),
            P("win", "space", None),
            P("win", None),
            P("win", None),
            P("win", None),
            P("win", None),
            P("win"),
            P("win"),
        ),
        out_specs=P("win", None, None),
        check_vma=False,
    )
```

```python
import jax
import jax.numpy as jnp
from jax import lax
from jax.experimental import pallas as pl
from jax.experimental.pallas import tpu as pltpu
from jax.sharding import PartitionSpec as P


K = 128
S = 256
WIN_DEV = 8
NCH = 2
TP = 1536


def coefficients(amp_re, amp_im, growth, freq, mode_count):
    steps = jnp.arange(S).astype(jnp.float32)
    live = (jnp.arange(K, dtype=jnp.int32)[None, :] < mode_count[:, None]).astype(jnp.float32)
    decay = jnp.exp(growth[:, :, None] * steps) * live[:, :, None]
    angle = freq[:, :, None] * steps
    cosine = jnp.cos(angle)
    sine = jnp.sin(angle)
    real_part = (amp_re[:, :, None] * cosine - amp_im[:, :, None] * sine) * decay
    imag_part = (amp_re[:, :, None] * sine + amp_im[:, :, None] * cosine) * decay
    stacked = jnp.stack([real_part, -imag_part], axis=2)
    return stacked.reshape(amp_re.shape[0], 2 * K, S).astype(jnp.bfloat16)


def gram_kernel(src_ref, s_ref, m_ref, c_ref, o_ref):
    t = pl.program_id(1)

    @pl.when(t == 0)
    def _():
        o_ref[...] = jnp.zeros_like(o_ref)

    s = s_ref[0].astype(jnp.float32)
    recon = jnp.dot(m_ref[0], c_ref[0], preferred_element_type=jnp.float32)
    r = (s - recon).astype(jnp.bfloat16)
    half = S // 2
    dims = (((0,), (0,)), ((), ()))
    top = lax.dot_general(r[:, :half], r, dims, preferred_element_type=jnp.float32)
    low = lax.dot_general(r[:, half:], r[:, half:], dims, preferred_element_type=jnp.float32)
    o_ref[0, :, : 2 * half] += top
    o_ref[0, :, 2 * half :] += low


def chunk_gram(source, snapshots, got, coef, chunk):
    nw, _, s = snapshots.shape
    rows = got.shape[1]
    tp = min(TP, rows)
    nt = rows // tp
    base = chunk * nt
    return pl.pallas_call(
        gram_kernel,
        grid_spec=pltpu.PrefetchScalarGridSpec(
            num_scalar_prefetch=1,
            grid=(nw, nt),
            in_specs=[
                pl.BlockSpec((1, tp, s), lambda p, t, src: (p, base + t, 0)),
                pl.BlockSpec((1, tp, s), lambda p, t, src: (src[p], t, 0)),
                pl.BlockSpec((1, s, s), lambda p, t, src: (p, 0, 0)),
            ],
            out_specs=pl.BlockSpec((1, s // 2, 3 * s // 2), lambda p, t, src: (p, 0, 0)),
        ),
        out_shape=jax.ShapeDtypeStruct((nw, s // 2, 3 * s // 2), jnp.float32),
        compiler_params=pltpu.CompilerParams(
            dimension_semantics=("arbitrary", "arbitrary"),
            vmem_limit_bytes=48 * 1024 * 1024,
        ),
        cost_estimate=pl.CostEstimate(
            flops=int(nw * rows * s * s * 2 * 1.75),
            bytes_accessed=int(nw * rows * s * 2 * 2),
            transcendentals=0,
        ),
    )(source, snapshots, got, coef)


def on_device(snapshots, modes, amp_re, amp_im, growth, freq, mode_count, slot_window):
    nblocks = lax.axis_size("win")
    me = lax.axis_index("win")
    nw, rows, s = snapshots.shape
    points_all = rows * lax.axis_size("space")

    dest = slot_window // WIN_DEV
    hit = dest[None, :] == jnp.arange(nblocks, dtype=jnp.int32)[:, None]
    pick = jnp.sum(jnp.where(hit, jnp.arange(nw, dtype=jnp.int32)[None, :], 0), axis=1)

    cp = rows // NCH
    gots = []
    for k in range(NCH):
        part = modes[:, k * cp : (k + 1) * cp, :]
        sendbuf = jnp.take(part, pick, axis=0, mode="clip")
        gots.append(lax.all_to_all(sendbuf, "win", split_axis=0, concat_axis=0, tiled=True))

    extra = jnp.zeros((nw, K), jnp.float32)
    extra = extra.at[:, 0].set(mode_count.astype(jnp.float32))
    extra = extra.at[:, 1].set(slot_window.astype(jnp.float32))
    packed = jnp.concatenate([amp_re, amp_im, growth, freq, extra], axis=1)
    packed_all = lax.all_gather(packed, "win", axis=0, tiled=True)
    sw_all = packed_all[:, 4 * K + 1].astype(jnp.int32)
    wins = me * WIN_DEV + jnp.arange(nw, dtype=jnp.int32)
    slot_ids = jnp.arange(packed_all.shape[0], dtype=jnp.int32)
    match = sw_all[None, :] == wins[:, None]
    slot = jnp.sum(jnp.where(match, slot_ids[None, :], 0), axis=1)
    source = slot // WIN_DEV
    sel = jnp.sum(jnp.where(match[:, :, None], packed_all[None, :, :], 0.0), axis=1)
    coef = coefficients(
        sel[:, 0:K],
        sel[:, K : 2 * K],
        sel[:, 2 * K : 3 * K],
        sel[:, 3 * K : 4 * K],
        sel[:, 4 * K].astype(jnp.int32),
    )

    part_sum = None
    for k in range(NCH):
        g = chunk_gram(source, snapshots, gots[k], coef, k)
        part_sum = g if part_sum is None else part_sum + g
    total = lax.psum(part_sum, "space") / points_all
    half = s // 2
    top = total[:, :, :s]
    mid = total[:, :, half:s]
    low = total[:, :, s:]
    bottom = jnp.concatenate([jnp.swapaxes(mid, 1, 2), low], axis=2)
    return jnp.concatenate([top, bottom], axis=1)


def solution(mesh):
    return jax.shard_map(
        on_device,
        mesh=mesh,
        in_specs=(
            P("win", "space", None),
            P("win", "space", None),
            P("win", None),
            P("win", None),
            P("win", None),
            P("win", None),
            P("win"),
            P("win"),
        ),
        out_specs=P("win", None, None),
        check_vma=False,
    )
```

```python
import jax
import jax.numpy as jnp
from jax import lax
from jax.experimental import pallas as pl
from jax.experimental.pallas import tpu as pltpu
from jax.sharding import PartitionSpec as P


K = 128
S = 256
WIN_DEV = 8
NCH = 2
TP = 1536


def coefficients(amp_re, amp_im, growth, freq, mode_count):
    steps = jnp.arange(S).astype(jnp.float32)
    live = (jnp.arange(K, dtype=jnp.int32)[None, :] < mode_count[:, None]).astype(jnp.float32)
    decay = jnp.exp(growth[:, :, None] * steps) * live[:, :, None]
    angle = freq[:, :, None] * steps
    cosine = jnp.cos(angle)
    sine = jnp.sin(angle)
    real_part = (amp_re[:, :, None] * cosine - amp_im[:, :, None] * sine) * decay
    imag_part = (amp_re[:, :, None] * sine + amp_im[:, :, None] * cosine) * decay
    stacked = jnp.stack([real_part, -imag_part], axis=2)
    return stacked.reshape(amp_re.shape[0], 2 * K, S).astype(jnp.bfloat16)


def gram_kernel(src_ref, s_ref, m_ref, c_ref, o_ref):
    t = pl.program_id(1)

    @pl.when(t == 0)
    def _():
        o_ref[...] = jnp.zeros_like(o_ref)

    s = s_ref[0].astype(jnp.float32)
    recon = jnp.dot(m_ref[0], c_ref[0], preferred_element_type=jnp.float32)
    r = (s - recon).astype(jnp.bfloat16)
    half = S // 2
    dims = (((0,), (0,)), ((), ()))
    top = lax.dot_general(r[:, :half], r, dims, preferred_element_type=jnp.float32)
    low = lax.dot_general(r[:, half:], r[:, half:], dims, preferred_element_type=jnp.float32)
    o_ref[0, :, : 2 * half] += top
    o_ref[0, :, 2 * half :] += low


def chunk_gram(source, snapshots, got, coef, chunk):
    nw, _, s = snapshots.shape
    rows = got.shape[1]
    tp = min(TP, rows)
    nt = rows // tp
    base = chunk * nt
    return pl.pallas_call(
        gram_kernel,
        grid_spec=pltpu.PrefetchScalarGridSpec(
            num_scalar_prefetch=1,
            grid=(nw, nt),
            in_specs=[
                pl.BlockSpec((1, tp, s), lambda p, t, src: (p, base + t, 0)),
                pl.BlockSpec((1, tp, s), lambda p, t, src: (src[p], t, 0)),
                pl.BlockSpec((1, s, s), lambda p, t, src: (p, 0, 0)),
            ],
            out_specs=pl.BlockSpec((1, s // 2, 3 * s // 2), lambda p, t, src: (p, 0, 0)),
        ),
        out_shape=jax.ShapeDtypeStruct((nw, s // 2, 3 * s // 2), jnp.float32),
        compiler_params=pltpu.CompilerParams(
            dimension_semantics=("arbitrary", "arbitrary"),
            vmem_limit_bytes=48 * 1024 * 1024,
        ),
        cost_estimate=pl.CostEstimate(
            flops=int(nw * rows * s * s * 2 * 1.75),
            bytes_accessed=int(nw * rows * s * 2 * 2),
            transcendentals=0,
        ),
    )(source, snapshots, got, coef)


def copy_kernel(pick_ref, m_ref, o_ref):
    o_ref[...] = m_ref[...]


def send_buffer(pick, modes, chunk, rows):
    nb = pick.shape[0]
    s = modes.shape[2]
    tq = min(TP, rows)
    nt = rows // tq
    base = chunk * nt
    return pl.pallas_call(
        copy_kernel,
        grid_spec=pltpu.PrefetchScalarGridSpec(
            num_scalar_prefetch=1,
            grid=(nb, nt),
            in_specs=[pl.BlockSpec((1, tq, s), lambda b, t, pk: (pk[b], base + t, 0))],
            out_specs=pl.BlockSpec((1, tq, s), lambda b, t, pk: (b, t, 0)),
        ),
        out_shape=jax.ShapeDtypeStruct((nb, rows, s), modes.dtype),
        compiler_params=pltpu.CompilerParams(dimension_semantics=("arbitrary", "arbitrary")),
        cost_estimate=pl.CostEstimate(flops=0, bytes_accessed=2 * nb * rows * s * 2, transcendentals=0),
    )(pick, modes)


def on_device(snapshots, modes, amp_re, amp_im, growth, freq, mode_count, slot_window):
    nblocks = lax.axis_size("win")
    me = lax.axis_index("win")
    nw, rows, s = snapshots.shape
    points_all = rows * lax.axis_size("space")

    dest = slot_window // WIN_DEV
    hit = dest[None, :] == jnp.arange(nblocks, dtype=jnp.int32)[:, None]
    pick = jnp.sum(jnp.where(hit, jnp.arange(nw, dtype=jnp.int32)[None, :], 0), axis=1)

    cp = rows // NCH
    gots = []
    for k in range(NCH):
        sendbuf = send_buffer(pick, modes, k, cp)
        gots.append(lax.all_to_all(sendbuf, "win", split_axis=0, concat_axis=0, tiled=True))

    extra = jnp.zeros((nw, K), jnp.float32)
    extra = extra.at[:, 0].set(mode_count.astype(jnp.float32))
    extra = extra.at[:, 1].set(slot_window.astype(jnp.float32))
    packed = jnp.concatenate([amp_re, amp_im, growth, freq, extra], axis=1)
    packed_all = lax.all_gather(packed, "win", axis=0, tiled=True)
    sw_all = packed_all[:, 4 * K + 1].astype(jnp.int32)
    wins = me * WIN_DEV + jnp.arange(nw, dtype=jnp.int32)
    slot_ids = jnp.arange(packed_all.shape[0], dtype=jnp.int32)
    match = sw_all[None, :] == wins[:, None]
    slot = jnp.sum(jnp.where(match, slot_ids[None, :], 0), axis=1)
    source = slot // WIN_DEV
    sel = jnp.sum(jnp.where(match[:, :, None], packed_all[None, :, :], 0.0), axis=1)
    coef = coefficients(
        sel[:, 0:K],
        sel[:, K : 2 * K],
        sel[:, 2 * K : 3 * K],
        sel[:, 3 * K : 4 * K],
        sel[:, 4 * K].astype(jnp.int32),
    )

    part_sum = None
    for k in range(NCH):
        g = chunk_gram(source, snapshots, gots[k], coef, k)
        part_sum = g if part_sum is None else part_sum + g
    total = lax.psum(part_sum, "space") / points_all
    half = s // 2
    top = total[:, :, :s]
    mid = total[:, :, half:s]
    low = total[:, :, s:]
    bottom = jnp.concatenate([jnp.swapaxes(mid, 1, 2), low], axis=2)
    return jnp.concatenate([top, bottom], axis=1)


def solution(mesh):
    return jax.shard_map(
        on_device,
        mesh=mesh,
        in_specs=(
            P("win", "space", None),
            P("win", "space", None),
            P("win", None),
            P("win", None),
            P("win", None),
            P("win", None),
            P("win"),
            P("win"),
        ),
        out_specs=P("win", None, None),
        check_vma=False,
    )
```

```python
import jax
import jax.numpy as jnp
from jax import lax
from jax.experimental import pallas as pl
from jax.experimental.pallas import tpu as pltpu
from jax.sharding import PartitionSpec as P


K = 128
S = 256
WIN_DEV = 8
NCH = 1
TP = 1536


def coefficients(amp_re, amp_im, growth, freq, mode_count):
    steps = jnp.arange(S).astype(jnp.float32)
    live = (jnp.arange(K, dtype=jnp.int32)[None, :] < mode_count[:, None]).astype(jnp.float32)
    decay = jnp.exp(growth[:, :, None] * steps) * live[:, :, None]
    angle = freq[:, :, None] * steps
    cosine = jnp.cos(angle)
    sine = jnp.sin(angle)
    real_part = (amp_re[:, :, None] * cosine - amp_im[:, :, None] * sine) * decay
    imag_part = (amp_re[:, :, None] * sine + amp_im[:, :, None] * cosine) * decay
    stacked = jnp.stack([real_part, -imag_part], axis=2)
    return stacked.reshape(amp_re.shape[0], 2 * K, S).astype(jnp.bfloat16)


def gram_kernel(src_ref, s_ref, m_ref, c_ref, o_ref):
    t = pl.program_id(1)

    @pl.when(t == 0)
    def _():
        o_ref[...] = jnp.zeros_like(o_ref)

    s = s_ref[0].astype(jnp.float32)
    recon = jnp.dot(m_ref[0], c_ref[0], preferred_element_type=jnp.float32)
    r = (s - recon).astype(jnp.bfloat16)
    half = S // 2
    dims = (((0,), (0,)), ((), ()))
    top = lax.dot_general(r[:, :half], r, dims, preferred_element_type=jnp.float32)
    low = lax.dot_general(r[:, half:], r[:, half:], dims, preferred_element_type=jnp.float32)
    o_ref[0, :, : 2 * half] += top
    o_ref[0, :, 2 * half :] += low


def chunk_gram(source, snapshots, got, coef, chunk):
    nw, _, s = snapshots.shape
    rows = got.shape[1]
    tp = min(TP, rows)
    nt = rows // tp
    base = chunk * nt
    return pl.pallas_call(
        gram_kernel,
        grid_spec=pltpu.PrefetchScalarGridSpec(
            num_scalar_prefetch=1,
            grid=(nw, nt),
            in_specs=[
                pl.BlockSpec((1, tp, s), lambda p, t, src: (p, base + t, 0)),
                pl.BlockSpec((1, tp, s), lambda p, t, src: (src[p], t, 0)),
                pl.BlockSpec((1, s, s), lambda p, t, src: (p, 0, 0)),
            ],
            out_specs=pl.BlockSpec((1, s // 2, 3 * s // 2), lambda p, t, src: (p, 0, 0)),
        ),
        out_shape=jax.ShapeDtypeStruct((nw, s // 2, 3 * s // 2), jnp.float32),
        compiler_params=pltpu.CompilerParams(
            dimension_semantics=("arbitrary", "arbitrary"),
            vmem_limit_bytes=48 * 1024 * 1024,
        ),
        cost_estimate=pl.CostEstimate(
            flops=int(nw * rows * s * s * 2 * 1.75),
            bytes_accessed=int(nw * rows * s * 2 * 2),
            transcendentals=0,
        ),
    )(source, snapshots, got, coef)


def copy_kernel(pick_ref, m_ref, o_ref):
    o_ref[...] = m_ref[...]


def send_buffer(pick, modes, chunk, rows):
    nb = pick.shape[0]
    s = modes.shape[2]
    tq = min(TP, rows)
    nt = rows // tq
    base = chunk * nt
    return pl.pallas_call(
        copy_kernel,
        grid_spec=pltpu.PrefetchScalarGridSpec(
            num_scalar_prefetch=1,
            grid=(nb, nt),
            in_specs=[pl.BlockSpec((1, tq, s), lambda b, t, pk: (pk[b], base + t, 0))],
            out_specs=pl.BlockSpec((1, tq, s), lambda b, t, pk: (b, t, 0)),
        ),
        out_shape=jax.ShapeDtypeStruct((nb, rows, s), modes.dtype),
        compiler_params=pltpu.CompilerParams(dimension_semantics=("arbitrary", "arbitrary")),
        cost_estimate=pl.CostEstimate(flops=0, bytes_accessed=2 * nb * rows * s * 2, transcendentals=0),
    )(pick, modes)


def on_device(snapshots, modes, amp_re, amp_im, growth, freq, mode_count, slot_window):
    nblocks = lax.axis_size("win")
    me = lax.axis_index("win")
    nw, rows, s = snapshots.shape
    points_all = rows * lax.axis_size("space")

    dest = slot_window // WIN_DEV
    hit = dest[None, :] == jnp.arange(nblocks, dtype=jnp.int32)[:, None]
    pick = jnp.sum(jnp.where(hit, jnp.arange(nw, dtype=jnp.int32)[None, :], 0), axis=1)

    cp = rows // NCH
    gots = []
    for k in range(NCH):
        if NCH == 1:
            sendbuf = jnp.take(modes, pick, axis=0, mode="clip")
        else:
            sendbuf = send_buffer(pick, modes, k, cp)
        gots.append(lax.all_to_all(sendbuf, "win", split_axis=0, concat_axis=0, tiled=True))

    extra = jnp.zeros((nw, K), jnp.float32)
    extra = extra.at[:, 0].set(mode_count.astype(jnp.float32))
    extra = extra.at[:, 1].set(slot_window.astype(jnp.float32))
    packed = jnp.concatenate([amp_re, amp_im, growth, freq, extra], axis=1)
    packed_all = lax.all_gather(packed, "win", axis=0, tiled=True)
    sw_all = packed_all[:, 4 * K + 1].astype(jnp.int32)
    wins = me * WIN_DEV + jnp.arange(nw, dtype=jnp.int32)
    slot_ids = jnp.arange(packed_all.shape[0], dtype=jnp.int32)
    match = sw_all[None, :] == wins[:, None]
    slot = jnp.sum(jnp.where(match, slot_ids[None, :], 0), axis=1)
    source = slot // WIN_DEV
    sel = jnp.sum(jnp.where(match[:, :, None], packed_all[None, :, :], 0.0), axis=1)
    coef = coefficients(
        sel[:, 0:K],
        sel[:, K : 2 * K],
        sel[:, 2 * K : 3 * K],
        sel[:, 3 * K : 4 * K],
        sel[:, 4 * K].astype(jnp.int32),
    )

    part_sum = None
    for k in range(NCH):
        g = chunk_gram(source, snapshots, gots[k], coef, k)
        part_sum = g if part_sum is None else part_sum + g
    total = lax.psum(part_sum, "space") / points_all
    half = s // 2
    top = total[:, :, :s]
    mid = total[:, :, half:s]
    low = total[:, :, s:]
    bottom = jnp.concatenate([jnp.swapaxes(mid, 1, 2), low], axis=2)
    return jnp.concatenate([top, bottom], axis=1)


def solution(mesh):
    return jax.shard_map(
        on_device,
        mesh=mesh,
        in_specs=(
            P("win", "space", None),
            P("win", "space", None),
            P("win", None),
            P("win", None),
            P("win", None),
            P("win", None),
            P("win"),
            P("win"),
        ),
        out_specs=P("win", None, None),
        check_vma=False,
    )
```

```python
import functools

import jax
import jax.numpy as jnp
from jax import lax
from jax.experimental import pallas as pl
from jax.experimental.pallas import tpu as pltpu
from jax.sharding import PartitionSpec as P


K = 128
S = 256
WIN_DEV = 8
NCH = 1
TP = 1536


def coefficients(amp_re, amp_im, growth, freq, mode_count):
    steps = jnp.arange(S).astype(jnp.float32)
    live = (jnp.arange(K, dtype=jnp.int32)[None, :] < mode_count[:, None]).astype(jnp.float32)
    decay = jnp.exp(growth[:, :, None] * steps) * live[:, :, None]
    angle = freq[:, :, None] * steps
    cosine = jnp.cos(angle)
    sine = jnp.sin(angle)
    real_part = (amp_re[:, :, None] * cosine - amp_im[:, :, None] * sine) * decay
    imag_part = (amp_re[:, :, None] * sine + amp_im[:, :, None] * cosine) * decay
    stacked = jnp.stack([real_part, -imag_part], axis=2)
    return stacked.reshape(amp_re.shape[0], 2 * K, S).astype(jnp.bfloat16)


def gram_kernel(src_ref, s_ref, m_ref, c_ref, o_ref):
    t = pl.program_id(1)

    @pl.when(t == 0)
    def _():
        o_ref[...] = jnp.zeros_like(o_ref)

    s = s_ref[0].astype(jnp.float32)
    recon = jnp.dot(m_ref[0], c_ref[0], preferred_element_type=jnp.float32)
    r = (s - recon).astype(jnp.bfloat16)
    half = S // 2
    dims = (((0,), (0,)), ((), ()))
    top = lax.dot_general(r[:, :half], r, dims, preferred_element_type=jnp.float32)
    low = lax.dot_general(r[:, half:], r[:, half:], dims, preferred_element_type=jnp.float32)
    o_ref[0, :, : 2 * half] += top
    o_ref[0, :, 2 * half :] += low


def chunk_gram(source, snapshots, got, coef, chunk):
    nw, _, s = snapshots.shape
    rows = got.shape[1]
    tp = min(TP, rows)
    nt = rows // tp
    base = chunk * nt
    return pl.pallas_call(
        gram_kernel,
        grid_spec=pltpu.PrefetchScalarGridSpec(
            num_scalar_prefetch=1,
            grid=(nw, nt),
            in_specs=[
                pl.BlockSpec((1, tp, s), lambda p, t, src: (p, base + t, 0)),
                pl.BlockSpec((1, tp, s), lambda p, t, src: (src[p], t, 0)),
                pl.BlockSpec((1, s, s), lambda p, t, src: (p, 0, 0)),
            ],
            out_specs=pl.BlockSpec((1, s // 2, 3 * s // 2), lambda p, t, src: (p, 0, 0)),
        ),
        out_shape=jax.ShapeDtypeStruct((nw, s // 2, 3 * s // 2), jnp.float32),
        compiler_params=pltpu.CompilerParams(
            dimension_semantics=("arbitrary", "arbitrary"),
            vmem_limit_bytes=48 * 1024 * 1024,
        ),
        cost_estimate=pl.CostEstimate(
            flops=int(nw * rows * s * s * 2 * 1.75),
            bytes_accessed=int(nw * rows * s * 2 * 2),
            transcendentals=0,
        ),
    )(source, snapshots, got, coef)


def copy_kernel(pick_ref, m_ref, o_ref):
    o_ref[...] = m_ref[...]


def send_buffer(pick, modes, chunk, rows):
    nb = pick.shape[0]
    s = modes.shape[2]
    tq = min(TP, rows)
    nt = rows // tq
    base = chunk * nt
    return pl.pallas_call(
        copy_kernel,
        grid_spec=pltpu.PrefetchScalarGridSpec(
            num_scalar_prefetch=1,
            grid=(nb, nt),
            in_specs=[pl.BlockSpec((1, tq, s), lambda b, t, pk: (pk[b], base + t, 0))],
            out_specs=pl.BlockSpec((1, tq, s), lambda b, t, pk: (b, t, 0)),
        ),
        out_shape=jax.ShapeDtypeStruct((nb, rows, s), modes.dtype),
        compiler_params=pltpu.CompilerParams(dimension_semantics=("arbitrary", "arbitrary")),
        cost_estimate=pl.CostEstimate(flops=0, bytes_accessed=2 * nb * rows * s * 2, transcendentals=0),
    )(pick, modes)


def exchange_kernel(sb_ref, pk_ref, out_ref, pall_ref, send_sem, recv_sem, psend_sem, precv_sem, own_sem):
    n = out_ref.shape[0]
    me = lax.axis_index("win")
    sp = lax.axis_index("space")
    mesh_id = pl.DeviceIdType.MESH

    barrier = pltpu.get_barrier_semaphore()
    for k in range(1, n):
        peer = lax.rem(me + k, n)
        pl.semaphore_signal(barrier, inc=1, device_id=(sp, peer), device_id_type=mesh_id)
    pl.semaphore_wait(barrier, n - 1)

    own = pltpu.make_async_copy(sb_ref.at[me], out_ref.at[me], own_sem.at[0])
    own.start()
    ownp = pltpu.make_async_copy(pk_ref, pall_ref.at[me], own_sem.at[1])
    ownp.start()
    copies = []
    for k in range(1, n):
        peer = lax.rem(me + k, n)
        pc = pltpu.make_async_remote_copy(
            src_ref=pk_ref,
            dst_ref=pall_ref.at[me],
            send_sem=psend_sem.at[k],
            recv_sem=precv_sem.at[k],
            device_id=(sp, peer),
            device_id_type=mesh_id,
        )
        pc.start()
        copies.append(pc)
    for k in range(1, n):
        peer = lax.rem(me + k, n)
        c = pltpu.make_async_remote_copy(
            src_ref=sb_ref.at[peer],
            dst_ref=out_ref.at[me],
            send_sem=send_sem.at[k],
            recv_sem=recv_sem.at[k],
            device_id=(sp, peer),
            device_id_type=mesh_id,
        )
        c.start()
        copies.append(c)
    own.wait()
    ownp.wait()
    for c in copies:
        c.wait()


def exchange(sendbuf, packed):
    n = sendbuf.shape[0]
    any_spec = pl.BlockSpec(memory_space=pl.ANY)
    return pl.pallas_call(
        exchange_kernel,
        in_specs=[any_spec, any_spec],
        out_specs=[any_spec, any_spec],
        out_shape=[
            jax.ShapeDtypeStruct(sendbuf.shape, sendbuf.dtype),
            jax.ShapeDtypeStruct((n,) + packed.shape, packed.dtype),
        ],
        scratch_shapes=[
            pltpu.SemaphoreType.DMA((n,)),
            pltpu.SemaphoreType.DMA((n,)),
            pltpu.SemaphoreType.DMA((n,)),
            pltpu.SemaphoreType.DMA((n,)),
            pltpu.SemaphoreType.DMA((2,)),
        ],
        compiler_params=pltpu.CompilerParams(collective_id=0, has_side_effects=True),
    )(sendbuf, packed)


def on_device(snapshots, modes, amp_re, amp_im, growth, freq, mode_count, slot_window):
    nblocks = lax.axis_size("win")
    me = lax.axis_index("win")
    nw, rows, s = snapshots.shape
    points_all = rows * lax.axis_size("space")

    dest = slot_window // WIN_DEV
    hit = dest[None, :] == jnp.arange(nblocks, dtype=jnp.int32)[:, None]
    pick = jnp.sum(jnp.where(hit, jnp.arange(nw, dtype=jnp.int32)[None, :], 0), axis=1)

    extra = jnp.zeros((nw, K), jnp.float32)
    extra = extra.at[:, 0].set(mode_count.astype(jnp.float32))
    extra = extra.at[:, 1].set(slot_window.astype(jnp.float32))
    packed = jnp.concatenate([amp_re, amp_im, growth, freq, extra], axis=1)
    sendbuf = jnp.take(modes, pick, axis=0, mode="clip")
    got, packed_all = exchange(sendbuf, packed)
    packed_all = packed_all.reshape((-1, packed.shape[1]))
    gots = [got]
    sw_all = packed_all[:, 4 * K + 1].astype(jnp.int32)
    wins = me * WIN_DEV + jnp.arange(nw, dtype=jnp.int32)
    slot_ids = jnp.arange(packed_all.shape[0], dtype=jnp.int32)
    match = sw_all[None, :] == wins[:, None]
    slot = jnp.sum(jnp.where(match, slot_ids[None, :], 0), axis=1)
    source = slot // WIN_DEV
    sel = jnp.sum(jnp.where(match[:, :, None], packed_all[None, :, :], 0.0), axis=1)
    coef = coefficients(
        sel[:, 0:K],
        sel[:, K : 2 * K],
        sel[:, 2 * K : 3 * K],
        sel[:, 3 * K : 4 * K],
        sel[:, 4 * K].astype(jnp.int32),
    )

    part_sum = None
    for k in range(NCH):
        g = chunk_gram(source, snapshots, gots[k], coef, k)
        part_sum = g if part_sum is None else part_sum + g
    total = lax.psum(part_sum, "space") / points_all
    half = s // 2
    top = total[:, :, :s]
    mid = total[:, :, half:s]
    low = total[:, :, s:]
    bottom = jnp.concatenate([jnp.swapaxes(mid, 1, 2), low], axis=2)
    return jnp.concatenate([top, bottom], axis=1)


def solution(mesh):
    return jax.shard_map(
        on_device,
        mesh=mesh,
        in_specs=(
            P("win", "space", None),
            P("win", "space", None),
            P("win", None),
            P("win", None),
            P("win", None),
            P("win", None),
            P("win"),
            P("win"),
        ),
        out_specs=P("win", None, None),
        check_vma=False,
    )
```

```python
import jax
import jax.numpy as jnp
from jax import lax
from jax.experimental import pallas as pl
from jax.experimental.pallas import tpu as pltpu
from jax.sharding import PartitionSpec as P


K = 128
S = 256
WIN_DEV = 8
NCH = 2
TP = 1536


def coefficients(amp_re, amp_im, growth, freq, mode_count):
    steps = jnp.arange(S).astype(jnp.float32)
    live = (jnp.arange(K, dtype=jnp.int32)[None, :] < mode_count[:, None]).astype(jnp.float32)
    decay = jnp.exp(growth[:, :, None] * steps) * live[:, :, None]
    angle = freq[:, :, None] * steps
    cosine = jnp.cos(angle)
    sine = jnp.sin(angle)
    real_part = (amp_re[:, :, None] * cosine - amp_im[:, :, None] * sine) * decay
    imag_part = (amp_re[:, :, None] * sine + amp_im[:, :, None] * cosine) * decay
    stacked = jnp.stack([real_part, -imag_part], axis=2)
    return stacked.reshape(amp_re.shape[0], 2 * K, S).astype(jnp.bfloat16)


def gram_kernel(src_ref, s_ref, m_ref, c_ref, o_ref):
    t = pl.program_id(1)

    @pl.when(t == 0)
    def _():
        o_ref[...] = jnp.zeros_like(o_ref)

    s = s_ref[0].astype(jnp.float32)
    recon = jnp.dot(m_ref[0], c_ref[0], preferred_element_type=jnp.float32)
    r = (s - recon).astype(jnp.bfloat16)
    half = S // 2
    dims = (((0,), (0,)), ((), ()))
    top = lax.dot_general(r[:, :half], r, dims, preferred_element_type=jnp.float32)
    low = lax.dot_general(r[:, half:], r[:, half:], dims, preferred_element_type=jnp.float32)
    o_ref[0, :, : 2 * half] += top
    o_ref[0, :, 2 * half :] += low


def chunk_gram(source, snapshots, got, coef, chunk):
    nw, _, s = snapshots.shape
    rows = got.shape[1]
    tp = min(TP, rows)
    nt = rows // tp
    base = chunk * nt
    return pl.pallas_call(
        gram_kernel,
        grid_spec=pltpu.PrefetchScalarGridSpec(
            num_scalar_prefetch=1,
            grid=(nw, nt),
            in_specs=[
                pl.BlockSpec((1, tp, s), lambda p, t, src: (p, base + t, 0)),
                pl.BlockSpec((1, tp, s), lambda p, t, src: (src[p], t, 0)),
                pl.BlockSpec((1, s, s), lambda p, t, src: (p, 0, 0)),
            ],
            out_specs=pl.BlockSpec((1, s // 2, 3 * s // 2), lambda p, t, src: (p, 0, 0)),
        ),
        out_shape=jax.ShapeDtypeStruct((nw, s // 2, 3 * s // 2), jnp.float32),
        compiler_params=pltpu.CompilerParams(
            dimension_semantics=("arbitrary", "arbitrary"),
            vmem_limit_bytes=48 * 1024 * 1024,
        ),
        cost_estimate=pl.CostEstimate(
            flops=int(nw * rows * s * s * 2 * 1.75),
            bytes_accessed=int(nw * rows * s * 2 * 2),
            transcendentals=0,
        ),
    )(source, snapshots, got, coef)


def on_device(snapshots, modes, amp_re, amp_im, growth, freq, mode_count, slot_window):
    nblocks = lax.axis_size("win")
    me = lax.axis_index("win")
    nw, rows, s = snapshots.shape
    points_all = rows * lax.axis_size("space")

    dest = slot_window // WIN_DEV
    hit = dest[None, :] == jnp.arange(nblocks, dtype=jnp.int32)[:, None]
    pick = jnp.sum(jnp.where(hit, jnp.arange(nw, dtype=jnp.int32)[None, :], 0), axis=1)

    cp = rows // NCH
    modes_r = modes.reshape(nw, NCH, cp, s)
    gots = []
    for k in range(NCH):
        sendbuf = modes_r[pick, k]
        gots.append(lax.all_to_all(sendbuf, "win", split_axis=0, concat_axis=0, tiled=True))

    extra = jnp.zeros((nw, K), jnp.float32)
    extra = extra.at[:, 0].set(mode_count.astype(jnp.float32))
    extra = extra.at[:, 1].set(slot_window.astype(jnp.float32))
    packed = jnp.concatenate([amp_re, amp_im, growth, freq, extra], axis=1)
    spread = jnp.zeros((nblocks,) + packed.shape, jnp.float32)
    spread = lax.dynamic_update_slice(spread, packed[None], (me, 0, 0))
    packed_all = lax.psum(spread, "win").reshape((-1, packed.shape[1]))
    sw_all = packed_all[:, 4 * K + 1].astype(jnp.int32)
    wins = me * WIN_DEV + jnp.arange(nw, dtype=jnp.int32)
    slot_ids = jnp.arange(packed_all.shape[0], dtype=jnp.int32)
    match = sw_all[None, :] == wins[:, None]
    slot = jnp.sum(jnp.where(match, slot_ids[None, :], 0), axis=1)
    source = slot // WIN_DEV
    sel = jnp.sum(jnp.where(match[:, :, None], packed_all[None, :, :], 0.0), axis=1)
    coef = coefficients(
        sel[:, 0:K],
        sel[:, K : 2 * K],
        sel[:, 2 * K : 3 * K],
        sel[:, 3 * K : 4 * K],
        sel[:, 4 * K].astype(jnp.int32),
    )

    part_sum = None
    for k in range(NCH):
        g = chunk_gram(source, snapshots, gots[k], coef, k)
        part_sum = g if part_sum is None else part_sum + g
    total = lax.psum(part_sum, "space") / points_all
    half = s // 2
    top = total[:, :, :s]
    mid = total[:, :, half:s]
    low = total[:, :, s:]
    bottom = jnp.concatenate([jnp.swapaxes(mid, 1, 2), low], axis=2)
    return jnp.concatenate([top, bottom], axis=1)


def solution(mesh):
    return jax.shard_map(
        on_device,
        mesh=mesh,
        in_specs=(
            P("win", "space", None),
            P("win", "space", None),
            P("win", None),
            P("win", None),
            P("win", None),
            P("win", None),
            P("win"),
            P("win"),
        ),
        out_specs=P("win", None, None),
        check_vma=False,
    )
```

```python
import functools

import jax
import jax.numpy as jnp
from jax import lax
from jax.experimental import pallas as pl
from jax.experimental.pallas import tpu as pltpu
from jax.sharding import PartitionSpec as P


K = 128
S = 256
WIN_DEV = 8
NCH = 1
TP = 1536


def coefficients(amp_re, amp_im, growth, freq, mode_count):
    steps = jnp.arange(S).astype(jnp.float32)
    live = (jnp.arange(K, dtype=jnp.int32)[None, :] < mode_count[:, None]).astype(jnp.float32)
    decay = jnp.exp(growth[:, :, None] * steps) * live[:, :, None]
    angle = freq[:, :, None] * steps
    cosine = jnp.cos(angle)
    sine = jnp.sin(angle)
    real_part = (amp_re[:, :, None] * cosine - amp_im[:, :, None] * sine) * decay
    imag_part = (amp_re[:, :, None] * sine + amp_im[:, :, None] * cosine) * decay
    stacked = jnp.stack([real_part, -imag_part], axis=2)
    return stacked.reshape(amp_re.shape[0], 2 * K, S).astype(jnp.bfloat16)


def gram_kernel(src_ref, s_ref, m_ref, c_ref, o_ref):
    t = pl.program_id(1)

    @pl.when(t == 0)
    def _():
        o_ref[...] = jnp.zeros_like(o_ref)

    s = s_ref[0].astype(jnp.float32)
    recon = jnp.dot(m_ref[0], c_ref[0], preferred_element_type=jnp.float32)
    r = (s - recon).astype(jnp.bfloat16)
    half = S // 2
    dims = (((0,), (0,)), ((), ()))
    top = lax.dot_general(r[:, :half], r, dims, preferred_element_type=jnp.float32)
    low = lax.dot_general(r[:, half:], r[:, half:], dims, preferred_element_type=jnp.float32)
    o_ref[0, :, : 2 * half] += top
    o_ref[0, :, 2 * half :] += low


def chunk_gram(source, snapshots, got, coef, chunk):
    nw, _, s = snapshots.shape
    rows = snapshots.shape[1] // NCH
    tp = min(TP, rows)
    nt = rows // tp
    base = chunk * nt
    return pl.pallas_call(
        gram_kernel,
        grid_spec=pltpu.PrefetchScalarGridSpec(
            num_scalar_prefetch=1,
            grid=(nw, nt),
            in_specs=[
                pl.BlockSpec((1, tp, s), lambda p, t, src: (p, base + t, 0)),
                pl.BlockSpec((1, tp, s), lambda p, t, src: (src[p], t, 0)),
                pl.BlockSpec((1, s, s), lambda p, t, src: (p, 0, 0)),
            ],
            out_specs=pl.BlockSpec((1, s // 2, 3 * s // 2), lambda p, t, src: (p, 0, 0)),
        ),
        out_shape=jax.ShapeDtypeStruct((nw, s // 2, 3 * s // 2), jnp.float32),
        compiler_params=pltpu.CompilerParams(
            dimension_semantics=("arbitrary", "arbitrary"),
            vmem_limit_bytes=48 * 1024 * 1024,
        ),
        cost_estimate=pl.CostEstimate(
            flops=int(nw * rows * s * s * 2 * 1.75),
            bytes_accessed=int(nw * rows * s * 2 * 2),
            transcendentals=0,
        ),
    )(source, snapshots, got, coef)


def copy_kernel(pick_ref, m_ref, o_ref):
    o_ref[...] = m_ref[...]


def send_buffer(pick, modes, chunk, rows):
    nb = pick.shape[0]
    s = modes.shape[2]
    tq = min(TP, rows)
    nt = rows // tq
    base = chunk * nt
    return pl.pallas_call(
        copy_kernel,
        grid_spec=pltpu.PrefetchScalarGridSpec(
            num_scalar_prefetch=1,
            grid=(nb, nt),
            in_specs=[pl.BlockSpec((1, tq, s), lambda b, t, pk: (pk[b], base + t, 0))],
            out_specs=pl.BlockSpec((1, tq, s), lambda b, t, pk: (b, t, 0)),
        ),
        out_shape=jax.ShapeDtypeStruct((nb, rows, s), modes.dtype),
        compiler_params=pltpu.CompilerParams(dimension_semantics=("arbitrary", "arbitrary")),
        cost_estimate=pl.CostEstimate(flops=0, bytes_accessed=2 * nb * rows * s * 2, transcendentals=0),
    )(pick, modes)


def on_device(snapshots, modes, amp_re, amp_im, growth, freq, mode_count, slot_window):
    nblocks = lax.axis_size("win")
    me = lax.axis_index("win")
    nw, rows, s = snapshots.shape
    points_all = rows * lax.axis_size("space")

    dest = slot_window // WIN_DEV
    hit = dest[None, :] == jnp.arange(nblocks, dtype=jnp.int32)[:, None]
    pick = jnp.sum(jnp.where(hit, jnp.arange(nw, dtype=jnp.int32)[None, :], 0), axis=1)

    prm = jnp.stack([amp_re, amp_im, growth, freq], axis=1)
    hi = lax.reduce_precision(prm, exponent_bits=8, mantissa_bits=7)
    rest = prm - hi
    mid = lax.reduce_precision(rest, exponent_bits=8, mantissa_bits=7)
    low = rest - mid
    parts = jnp.stack([hi, mid, low], axis=1).astype(jnp.bfloat16).reshape(nw, 6, s)
    ints = jnp.zeros((nw, 2, s), jnp.float32)
    ints = ints.at[:, 0, 0].set(mode_count.astype(jnp.float32))
    ints = ints.at[:, 0, 1].set(slot_window.astype(jnp.float32))
    prows = jnp.concatenate([parts, ints.astype(jnp.bfloat16)], axis=1)
    payload = jnp.concatenate([modes, prows], axis=1)
    sendbuf = jnp.take(payload, pick, axis=0, mode="clip")
    got = lax.all_to_all(sendbuf, "win", split_axis=0, concat_axis=0, tiled=True)
    gots = [got]

    tail = got[:, rows:, :].astype(jnp.float32)
    sw_got = tail[:, 6, 1].astype(jnp.int32)
    wins = me * WIN_DEV + jnp.arange(nw, dtype=jnp.int32)
    srcs = jnp.arange(nblocks, dtype=jnp.int32)
    match = sw_got[None, :] == wins[:, None]
    source = jnp.sum(jnp.where(match, srcs[None, :], 0), axis=1)
    sel = jnp.sum(jnp.where(match[:, :, None, None], tail[None], 0.0), axis=1)
    trip = sel[:, :6, :].reshape(nw, 3, 4, K)
    prm_sel = (trip[:, 0] + trip[:, 1]) + trip[:, 2]
    coef = coefficients(
        prm_sel[:, 0],
        prm_sel[:, 1],
        prm_sel[:, 2],
        prm_sel[:, 3],
        sel[:, 6, 0].astype(jnp.int32),
    )

    part_sum = None
    for k in range(NCH):
        g = chunk_gram(source, snapshots, gots[k], coef, k)
        part_sum = g if part_sum is None else part_sum + g
    total = lax.psum(part_sum, "space") / points_all
    half = s // 2
    top = total[:, :, :s]
    mid = total[:, :, half:s]
    low = total[:, :, s:]
    bottom = jnp.concatenate([jnp.swapaxes(mid, 1, 2), low], axis=2)
    return jnp.concatenate([top, bottom], axis=1)


def solution(mesh):
    return jax.shard_map(
        on_device,
        mesh=mesh,
        in_specs=(
            P("win", "space", None),
            P("win", "space", None),
            P("win", None),
            P("win", None),
            P("win", None),
            P("win", None),
            P("win"),
            P("win"),
        ),
        out_specs=P("win", None, None),
        check_vma=False,
    )
```

```python
import jax
import jax.numpy as jnp
from jax import lax
from jax.experimental import pallas as pl
from jax.experimental.pallas import tpu as pltpu
from jax.sharding import PartitionSpec as P


K = 128
S = 256
WIN_DEV = 8
NCH = 2
TP = 1536


def coefficients(amp_re, amp_im, growth, freq, mode_count):
    steps = jnp.arange(S).astype(jnp.float32)
    live = (jnp.arange(K, dtype=jnp.int32)[None, :] < mode_count[:, None]).astype(jnp.float32)
    decay = jnp.exp(growth[:, :, None] * steps) * live[:, :, None]
    angle = freq[:, :, None] * steps
    cosine = jnp.cos(angle)
    sine = jnp.sin(angle)
    real_part = (amp_re[:, :, None] * cosine - amp_im[:, :, None] * sine) * decay
    imag_part = (amp_re[:, :, None] * sine + amp_im[:, :, None] * cosine) * decay
    stacked = jnp.stack([real_part, -imag_part], axis=2)
    return stacked.reshape(amp_re.shape[0], 2 * K, S).astype(jnp.bfloat16)


def gram_kernel(src_ref, s_ref, m_ref, c_ref, o_ref):
    t = pl.program_id(1)

    @pl.when(t == 0)
    def _():
        o_ref[...] = jnp.zeros_like(o_ref)

    s = s_ref[0].astype(jnp.float32)
    recon = jnp.dot(m_ref[0], c_ref[0], preferred_element_type=jnp.float32)
    r = (s - recon).astype(jnp.bfloat16)
    half = S // 2
    dims = (((0,), (0,)), ((), ()))
    top = lax.dot_general(r[:, :half], r, dims, preferred_element_type=jnp.float32)
    low = lax.dot_general(r[:, half:], r[:, half:], dims, preferred_element_type=jnp.float32)
    o_ref[0, :, : 2 * half] += top
    o_ref[0, :, 2 * half :] += low


def chunk_gram(source, snapshots, got, coef, chunk):
    nw, _, s = snapshots.shape
    rows = got.shape[1]
    tp = min(TP, rows)
    nt = rows // tp
    base = chunk * nt
    return pl.pallas_call(
        gram_kernel,
        grid_spec=pltpu.PrefetchScalarGridSpec(
            num_scalar_prefetch=1,
            grid=(nw, nt),
            in_specs=[
                pl.BlockSpec((1, tp, s), lambda p, t, src: (p, base + t, 0)),
                pl.BlockSpec((1, tp, s), lambda p, t, src: (src[p], t, 0)),
                pl.BlockSpec((1, s, s), lambda p, t, src: (p, 0, 0)),
            ],
            out_specs=pl.BlockSpec((1, s // 2, 3 * s // 2), lambda p, t, src: (p, 0, 0)),
        ),
        out_shape=jax.ShapeDtypeStruct((nw, s // 2, 3 * s // 2), jnp.float32),
        compiler_params=pltpu.CompilerParams(
            dimension_semantics=("arbitrary", "arbitrary"),
            vmem_limit_bytes=48 * 1024 * 1024,
        ),
        cost_estimate=pl.CostEstimate(
            flops=int(nw * rows * s * s * 2 * 1.75),
            bytes_accessed=int(nw * rows * s * 2 * 2),
            transcendentals=0,
        ),
    )(source, snapshots, got, coef)


def on_device(snapshots, modes, amp_re, amp_im, growth, freq, mode_count, slot_window):
    nblocks = lax.axis_size("win")
    me = lax.axis_index("win")
    nw, rows, s = snapshots.shape
    points_all = rows * lax.axis_size("space")

    dest = slot_window // WIN_DEV
    hit = dest[None, :] == jnp.arange(nblocks, dtype=jnp.int32)[:, None]
    pick = jnp.sum(jnp.where(hit, jnp.arange(nw, dtype=jnp.int32)[None, :], 0), axis=1)

    cp = rows // NCH
    modes_r = modes.reshape(nw, NCH, cp, s)
    gots = []
    for k in range(NCH):
        sendbuf = modes_r[pick, k]
        gots.append(lax.all_to_all(sendbuf, "win", split_axis=0, concat_axis=0, tiled=True))

    extra = jnp.zeros((nw, K), jnp.float32)
    extra = extra.at[:, 0].set(mode_count.astype(jnp.float32))
    extra = extra.at[:, 1].set(slot_window.astype(jnp.float32))
    packed = jnp.concatenate([amp_re, amp_im, growth, freq, extra], axis=1)
    packed_all = lax.all_gather(packed, "win", axis=0, tiled=True)
    sw_all = packed_all[:, 4 * K + 1].astype(jnp.int32)
    wins = me * WIN_DEV + jnp.arange(nw, dtype=jnp.int32)
    slot_ids = jnp.arange(packed_all.shape[0], dtype=jnp.int32)
    match = sw_all[None, :] == wins[:, None]
    slot = jnp.sum(jnp.where(match, slot_ids[None, :], 0), axis=1)
    source = slot // WIN_DEV
    sel = jnp.sum(jnp.where(match[:, :, None], packed_all[None, :, :], 0.0), axis=1)
    coef = coefficients(
        sel[:, 0:K],
        sel[:, K : 2 * K],
        sel[:, 2 * K : 3 * K],
        sel[:, 3 * K : 4 * K],
        sel[:, 4 * K].astype(jnp.int32),
    )

    part_sum = None
    for k in range(NCH):
        g = chunk_gram(source, snapshots, gots[k], coef, k)
        part_sum = g if part_sum is None else part_sum + g
    nsp = lax.axis_size("space")
    mine = lax.all_to_all(part_sum, "space", split_axis=0, concat_axis=0, tiled=True)
    red = jnp.sum(mine.reshape((nsp, nw // nsp) + mine.shape[1:]), axis=0)
    spread = jnp.broadcast_to(red[None], (nsp,) + red.shape).reshape((nsp * red.shape[0],) + red.shape[1:])
    total = lax.all_to_all(spread, "space", split_axis=0, concat_axis=0, tiled=True) / points_all
    half = s // 2
    top = total[:, :, :s]
    mid = total[:, :, half:s]
    low = total[:, :, s:]
    bottom = jnp.concatenate([jnp.swapaxes(mid, 1, 2), low], axis=2)
    return jnp.concatenate([top, bottom], axis=1)


def solution(mesh):
    return jax.shard_map(
        on_device,
        mesh=mesh,
        in_specs=(
            P("win", "space", None),
            P("win", "space", None),
            P("win", None),
            P("win", None),
            P("win", None),
            P("win", None),
            P("win"),
            P("win"),
        ),
        out_specs=P("win", None, None),
        check_vma=False,
    )
```

```python
import jax
import jax.numpy as jnp
from jax import lax
from jax.experimental import pallas as pl
from jax.experimental.pallas import tpu as pltpu
from jax.sharding import PartitionSpec as P


K = 128
S = 256
WIN_DEV = 8
NCH = 2
TP = 1536


def coefficients(amp_re, amp_im, growth, freq, mode_count):
    steps = jnp.arange(S).astype(jnp.float32)
    live = (jnp.arange(K, dtype=jnp.int32)[None, :] < mode_count[:, None]).astype(jnp.float32)
    decay = jnp.exp(growth[:, :, None] * steps) * live[:, :, None]
    angle = freq[:, :, None] * steps
    cosine = jnp.cos(angle)
    sine = jnp.sin(angle)
    real_part = (amp_re[:, :, None] * cosine - amp_im[:, :, None] * sine) * decay
    imag_part = (amp_re[:, :, None] * sine + amp_im[:, :, None] * cosine) * decay
    stacked = jnp.stack([real_part, -imag_part], axis=2)
    return stacked.reshape(amp_re.shape[0], 2 * K, S).astype(jnp.bfloat16)


def gram_kernel(src_ref, s_ref, m_ref, c_ref, o_ref):
    t = pl.program_id(1)

    @pl.when(t == 0)
    def _():
        o_ref[...] = jnp.zeros_like(o_ref)

    s = s_ref[0].astype(jnp.float32)
    recon = jnp.dot(m_ref[0], c_ref[0], preferred_element_type=jnp.float32)
    r = (s - recon).astype(jnp.bfloat16)
    half = S // 2
    dims = (((0,), (0,)), ((), ()))
    top = lax.dot_general(r[:, :half], r, dims, preferred_element_type=jnp.float32)
    low = lax.dot_general(r[:, half:], r[:, half:], dims, preferred_element_type=jnp.float32)
    o_ref[0, :, : 2 * half] += top
    o_ref[0, :, 2 * half :] += low


def chunk_gram(source, snapshots, got, coef, chunk):
    nw, _, s = snapshots.shape
    rows = got.shape[1]
    tp = min(TP, rows)
    nt = rows // tp
    base = chunk * nt
    return pl.pallas_call(
        gram_kernel,
        grid_spec=pltpu.PrefetchScalarGridSpec(
            num_scalar_prefetch=1,
            grid=(nw, nt),
            in_specs=[
                pl.BlockSpec((1, tp, s), lambda p, t, src: (p, base + t, 0)),
                pl.BlockSpec((1, tp, s), lambda p, t, src: (src[p], t, 0)),
                pl.BlockSpec((1, s, s), lambda p, t, src: (p, 0, 0)),
            ],
            out_specs=pl.BlockSpec((1, s // 2, 3 * s // 2), lambda p, t, src: (p, 0, 0)),
        ),
        out_shape=jax.ShapeDtypeStruct((nw, s // 2, 3 * s // 2), jnp.float32),
        compiler_params=pltpu.CompilerParams(
            dimension_semantics=("arbitrary", "arbitrary"),
            vmem_limit_bytes=48 * 1024 * 1024,
        ),
        cost_estimate=pl.CostEstimate(
            flops=int(nw * rows * s * s * 2 * 1.75),
            bytes_accessed=int(nw * rows * s * 2 * 2),
            transcendentals=0,
        ),
    )(source, snapshots, got, coef)


def on_device(snapshots, modes, amp_re, amp_im, growth, freq, mode_count, slot_window):
    nblocks = lax.axis_size("win")
    me = lax.axis_index("win")
    nw, rows, s = snapshots.shape
    points_all = rows * lax.axis_size("space")

    dest = slot_window // WIN_DEV
    hit = dest[None, :] == jnp.arange(nblocks, dtype=jnp.int32)[:, None]
    pick = jnp.sum(jnp.where(hit, jnp.arange(nw, dtype=jnp.int32)[None, :], 0), axis=1)

    cp = rows // NCH
    modes_r = modes.reshape(nw, NCH, cp, s)
    gots = []
    for k in range(NCH):
        sendbuf = modes_r[pick, k]
        gots.append(lax.all_to_all(sendbuf, "win", split_axis=0, concat_axis=0, tiled=True))

    extra = jnp.zeros((nw, K), jnp.float32)
    extra = extra.at[:, 0].set(mode_count.astype(jnp.float32))
    extra = extra.at[:, 1].set(slot_window.astype(jnp.float32))
    packed = jnp.concatenate([amp_re, amp_im, growth, freq, extra], axis=1)
    packed_all = lax.all_gather(packed, "win", axis=0, tiled=True)
    sw_all = packed_all[:, 4 * K + 1].astype(jnp.int32)
    wins = me * WIN_DEV + jnp.arange(nw, dtype=jnp.int32)
    slot_ids = jnp.arange(packed_all.shape[0], dtype=jnp.int32)
    match = sw_all[None, :] == wins[:, None]
    slot = jnp.sum(jnp.where(match, slot_ids[None, :], 0), axis=1)
    source = slot // WIN_DEV
    sel = jnp.sum(jnp.where(match[:, :, None], packed_all[None, :, :], 0.0), axis=1)
    coef = coefficients(
        sel[:, 0:K],
        sel[:, K : 2 * K],
        sel[:, 2 * K : 3 * K],
        sel[:, 3 * K : 4 * K],
        sel[:, 4 * K].astype(jnp.int32),
    )

    part_sum = None
    for k in range(NCH):
        g = chunk_gram(source, snapshots, gots[k], coef, k)
        part_sum = g if part_sum is None else part_sum + g
    half = s // 2
    blk_a = part_sum[:, :, :half]
    blk_b = part_sum[:, :, half:s]
    blk_d = part_sum[:, :, s:]
    ii = jnp.arange(half, dtype=jnp.int32)[:, None]
    jj = jnp.arange(half, dtype=jnp.int32)[None, :]
    upper = ii <= jj
    merged = jnp.where(upper[None], blk_a, blk_d)
    diag_d = jnp.sum(jnp.where((ii == jj)[None], blk_d, 0.0), axis=1)
    extra_row = jnp.concatenate([diag_d, jnp.zeros_like(diag_d)], axis=1)[:, None, :]
    packed_g = jnp.concatenate([jnp.concatenate([blk_b, merged], axis=2), extra_row], axis=1)

    nsp = lax.axis_size("space")
    mine = lax.all_to_all(packed_g, "space", split_axis=0, concat_axis=0, tiled=True)
    red = jnp.sum(mine.reshape((nsp, nw // nsp) + mine.shape[1:]), axis=0)
    spread = jnp.broadcast_to(red[None], (nsp,) + red.shape).reshape((nsp * red.shape[0],) + red.shape[1:])
    total = lax.all_to_all(spread, "space", split_axis=0, concat_axis=0, tiled=True) / points_all

    tb = total[:, :half, :half]
    tm = total[:, :half, half:]
    tmt = jnp.swapaxes(tm, 1, 2)
    tdiag = total[:, half, :half]
    ta = jnp.where(upper[None], tm, tmt)
    td = jnp.where((ii > jj)[None], tm, jnp.where((ii < jj)[None], tmt, tdiag[:, None, :]))
    top = jnp.concatenate([ta, tb], axis=2)
    bottom = jnp.concatenate([jnp.swapaxes(tb, 1, 2), td], axis=2)
    return jnp.concatenate([top, bottom], axis=1)


def solution(mesh):
    return jax.shard_map(
        on_device,
        mesh=mesh,
        in_specs=(
            P("win", "space", None),
            P("win", "space", None),
            P("win", None),
            P("win", None),
            P("win", None),
            P("win", None),
            P("win"),
            P("win"),
        ),
        out_specs=P("win", None, None),
        check_vma=False,
    )
```

```python
import jax
import jax.numpy as jnp
from jax import lax
from jax.experimental import pallas as pl
from jax.experimental.pallas import tpu as pltpu
from jax.sharding import PartitionSpec as P


K = 128
S = 256
WIN_DEV = 8
NCH = 2
TP = 768


def coefficients(amp_re, amp_im, growth, freq, mode_count):
    steps = jnp.arange(S).astype(jnp.float32)
    live = (jnp.arange(K, dtype=jnp.int32)[None, :] < mode_count[:, None]).astype(jnp.float32)
    decay = jnp.exp(growth[:, :, None] * steps) * live[:, :, None]
    angle = freq[:, :, None] * steps
    cosine = jnp.cos(angle)
    sine = jnp.sin(angle)
    real_part = (amp_re[:, :, None] * cosine - amp_im[:, :, None] * sine) * decay
    imag_part = (amp_re[:, :, None] * sine + amp_im[:, :, None] * cosine) * decay
    stacked = jnp.stack([real_part, -imag_part], axis=2)
    return stacked.reshape(amp_re.shape[0], 2 * K, S).astype(jnp.bfloat16)


def gram_kernel(src_ref, s_ref, m_ref, c_ref, o_ref):
    t = pl.program_id(1)

    @pl.when(t == 0)
    def _():
        o_ref[...] = jnp.zeros_like(o_ref)

    s = s_ref[0].astype(jnp.float32)
    recon = jnp.dot(m_ref[0], c_ref[0], preferred_element_type=jnp.float32)
    r = (s - recon).astype(jnp.bfloat16)
    half = S // 2
    dims = (((0,), (0,)), ((), ()))
    top = lax.dot_general(r[:, :half], r, dims, preferred_element_type=jnp.float32)
    low = lax.dot_general(r[:, half:], r[:, half:], dims, preferred_element_type=jnp.float32)
    o_ref[0, :, : 2 * half] += top
    o_ref[0, :, 2 * half :] += low


def chunk_gram(source, snapshots, got, coef, chunk):
    nw, _, s = snapshots.shape
    rows = got.shape[1]
    tp = min(TP, rows)
    nt = rows // tp
    base = chunk * nt
    return pl.pallas_call(
        gram_kernel,
        grid_spec=pltpu.PrefetchScalarGridSpec(
            num_scalar_prefetch=1,
            grid=(nw, nt),
            in_specs=[
                pl.BlockSpec((1, tp, s), lambda p, t, src: (p, base + t, 0)),
                pl.BlockSpec((1, tp, s), lambda p, t, src: (src[p], t, 0)),
                pl.BlockSpec((1, s, s), lambda p, t, src: (p, 0, 0)),
            ],
            out_specs=pl.BlockSpec((1, s // 2, 3 * s // 2), lambda p, t, src: (p, 0, 0)),
        ),
        out_shape=jax.ShapeDtypeStruct((nw, s // 2, 3 * s // 2), jnp.float32),
        compiler_params=pltpu.CompilerParams(
            dimension_semantics=("arbitrary", "arbitrary"),
            vmem_limit_bytes=48 * 1024 * 1024,
        ),
        cost_estimate=pl.CostEstimate(
            flops=int(nw * rows * s * s * 2 * 1.75),
            bytes_accessed=int(nw * rows * s * 2 * 2),
            transcendentals=0,
        ),
    )(source, snapshots, got, coef)


def on_device(snapshots, modes, amp_re, amp_im, growth, freq, mode_count, slot_window):
    nblocks = lax.axis_size("win")
    me = lax.axis_index("win")
    nw, rows, s = snapshots.shape
    points_all = rows * lax.axis_size("space")

    dest = slot_window // WIN_DEV
    hit = dest[None, :] == jnp.arange(nblocks, dtype=jnp.int32)[:, None]
    pick = jnp.sum(jnp.where(hit, jnp.arange(nw, dtype=jnp.int32)[None, :], 0), axis=1)

    cp = rows // NCH
    modes_r = modes.reshape(nw, NCH, cp, s)
    gots = []
    for k in range(NCH):
        sendbuf = modes_r[pick, k]
        gots.append(lax.all_to_all(sendbuf, "win", split_axis=0, concat_axis=0, tiled=True))

    extra = jnp.zeros((nw, K), jnp.float32)
    extra = extra.at[:, 0].set(mode_count.astype(jnp.float32))
    extra = extra.at[:, 1].set(slot_window.astype(jnp.float32))
    packed = jnp.concatenate([amp_re, amp_im, growth, freq, extra], axis=1)
    packed_all = lax.all_gather(packed, "win", axis=0, tiled=True)
    sw_all = packed_all[:, 4 * K + 1].astype(jnp.int32)
    wins = me * WIN_DEV + jnp.arange(nw, dtype=jnp.int32)
    slot_ids = jnp.arange(packed_all.shape[0], dtype=jnp.int32)
    match = sw_all[None, :] == wins[:, None]
    slot = jnp.sum(jnp.where(match, slot_ids[None, :], 0), axis=1)
    source = slot // WIN_DEV
    sel = jnp.sum(jnp.where(match[:, :, None], packed_all[None, :, :], 0.0), axis=1)
    coef = coefficients(
        sel[:, 0:K],
        sel[:, K : 2 * K],
        sel[:, 2 * K : 3 * K],
        sel[:, 3 * K : 4 * K],
        sel[:, 4 * K].astype(jnp.int32),
    )

    part_sum = None
    for k in range(NCH):
        g = chunk_gram(source, snapshots, gots[k], coef, k)
        part_sum = g if part_sum is None else part_sum + g
    half = s // 2
    blk_a = part_sum[:, :, :half]
    blk_b = part_sum[:, :, half:s]
    blk_d = part_sum[:, :, s:]
    ii = jnp.arange(half, dtype=jnp.int32)[:, None]
    jj = jnp.arange(half, dtype=jnp.int32)[None, :]
    upper = ii <= jj
    merged = jnp.where(upper[None], blk_a, blk_d)
    diag_d = jnp.sum(jnp.where((ii == jj)[None], blk_d, 0.0), axis=1)
    extra_row = jnp.concatenate([diag_d, jnp.zeros_like(diag_d)], axis=1)[:, None, :]
    packed_g = jnp.concatenate([jnp.concatenate([blk_b, merged], axis=2), extra_row], axis=1)

    nsp = lax.axis_size("space")
    mine = lax.all_to_all(packed_g, "space", split_axis=0, concat_axis=0, tiled=True)
    red = jnp.sum(mine.reshape((nsp, nw // nsp) + mine.shape[1:]), axis=0) / points_all
    spread = jnp.broadcast_to(red[None], (nsp,) + red.shape).reshape((nsp * red.shape[0],) + red.shape[1:])
    total = lax.all_to_all(spread, "space", split_axis=0, concat_axis=0, tiled=True)

    tb = total[:, :half, :half]
    tm = total[:, :half, half:]
    tmt = jnp.swapaxes(tm, 1, 2)
    tdiag = total[:, half, :half]
    ta = jnp.where(upper[None], tm, tmt)
    td = jnp.where((ii > jj)[None], tm, jnp.where((ii < jj)[None], tmt, tdiag[:, None, :]))
    top = jnp.concatenate([ta, tb], axis=2)
    bottom = jnp.concatenate([jnp.swapaxes(tb, 1, 2), td], axis=2)
    return jnp.concatenate([top, bottom], axis=1)


def solution(mesh):
    return jax.shard_map(
        on_device,
        mesh=mesh,
        in_specs=(
            P("win", "space", None),
            P("win", "space", None),
            P("win", None),
            P("win", None),
            P("win", None),
            P("win", None),
            P("win"),
            P("win"),
        ),
        out_specs=P("win", None, None),
        check_vma=False,
    )
```

```python
import jax
import jax.numpy as jnp
from jax import lax
from jax.experimental import pallas as pl
from jax.experimental.pallas import tpu as pltpu
from jax.sharding import PartitionSpec as P


K = 128
S = 256
WIN_DEV = 8
NCH = 2
TP = 3072


def coefficients(amp_re, amp_im, growth, freq, mode_count):
    steps = jnp.arange(S).astype(jnp.float32)
    live = (jnp.arange(K, dtype=jnp.int32)[None, :] < mode_count[:, None]).astype(jnp.float32)
    decay = jnp.exp(growth[:, :, None] * steps) * live[:, :, None]
    angle = freq[:, :, None] * steps
    cosine = jnp.cos(angle)
    sine = jnp.sin(angle)
    real_part = (amp_re[:, :, None] * cosine - amp_im[:, :, None] * sine) * decay
    imag_part = (amp_re[:, :, None] * sine + amp_im[:, :, None] * cosine) * decay
    stacked = jnp.stack([real_part, -imag_part], axis=2)
    return stacked.reshape(amp_re.shape[0], 2 * K, S).astype(jnp.bfloat16)


def gram_kernel(src_ref, s_ref, m_ref, c_ref, o_ref):
    t = pl.program_id(1)

    @pl.when(t == 0)
    def _():
        o_ref[...] = jnp.zeros_like(o_ref)

    s = s_ref[0].astype(jnp.float32)
    recon = jnp.dot(m_ref[0], c_ref[0], preferred_element_type=jnp.float32)
    r = (s - recon).astype(jnp.bfloat16)
    half = S // 2
    dims = (((0,), (0,)), ((), ()))
    top = lax.dot_general(r[:, :half], r, dims, preferred_element_type=jnp.float32)
    low = lax.dot_general(r[:, half:], r[:, half:], dims, preferred_element_type=jnp.float32)
    o_ref[0, :, : 2 * half] += top
    o_ref[0, :, 2 * half :] += low


def chunk_gram(source, snapshots, got, coef, chunk):
    nw, _, s = snapshots.shape
    rows = snapshots.shape[1] // NCH
    tp = min(TP, rows)
    nt = rows // tp
    base = chunk * nt
    return pl.pallas_call(
        gram_kernel,
        grid_spec=pltpu.PrefetchScalarGridSpec(
            num_scalar_prefetch=1,
            grid=(nw, nt),
            in_specs=[
                pl.BlockSpec((1, tp, s), lambda p, t, src: (p, base + t, 0)),
                pl.BlockSpec((1, tp, s), lambda p, t, src: (src[p], t, 0)),
                pl.BlockSpec((1, s, s), lambda p, t, src: (p, 0, 0)),
            ],
            out_specs=pl.BlockSpec((1, s // 2, 3 * s // 2), lambda p, t, src: (p, 0, 0)),
        ),
        out_shape=jax.ShapeDtypeStruct((nw, s // 2, 3 * s // 2), jnp.float32),
        compiler_params=pltpu.CompilerParams(
            dimension_semantics=("arbitrary", "arbitrary"),
            vmem_limit_bytes=48 * 1024 * 1024,
        ),
        cost_estimate=pl.CostEstimate(
            flops=int(nw * rows * s * s * 2 * 1.75),
            bytes_accessed=int(nw * rows * s * 2 * 2),
            transcendentals=0,
        ),
    )(source, snapshots, got, coef)


def on_device(snapshots, modes, amp_re, amp_im, growth, freq, mode_count, slot_window):
    nblocks = lax.axis_size("win")
    me = lax.axis_index("win")
    nw, rows, s = snapshots.shape
    points_all = rows * lax.axis_size("space")

    dest = slot_window // WIN_DEV
    hit = dest[None, :] == jnp.arange(nblocks, dtype=jnp.int32)[:, None]
    pick = jnp.sum(jnp.where(hit, jnp.arange(nw, dtype=jnp.int32)[None, :], 0), axis=1)

    prm = jnp.stack([amp_re, amp_im, growth, freq], axis=1)
    hi = lax.reduce_precision(prm, exponent_bits=8, mantissa_bits=7)
    rest = prm - hi
    mid = lax.reduce_precision(rest, exponent_bits=8, mantissa_bits=7)
    low = rest - mid
    parts = jnp.stack([hi, mid, low], axis=1).astype(jnp.bfloat16).reshape(nw, 6, s)
    ints = jnp.zeros((nw, 2, s), jnp.float32)
    ints = ints.at[:, 0, 0].set(mode_count.astype(jnp.float32))
    ints = ints.at[:, 0, 1].set(slot_window.astype(jnp.float32))
    prows = jnp.concatenate([parts, ints.astype(jnp.bfloat16)], axis=1)

    cp = rows // NCH
    modes_r = modes.reshape(nw, NCH, cp, s)
    gots = []
    for k in range(NCH):
        sendbuf = modes_r[pick, k]
        if k == 0:
            sendbuf = jnp.concatenate([sendbuf, jnp.take(prows, pick, axis=0, mode="clip")], axis=1)
        gots.append(lax.all_to_all(sendbuf, "win", split_axis=0, concat_axis=0, tiled=True))

    tail = gots[0][:, cp:, :].astype(jnp.float32)
    sw_got = tail[:, 6, 1].astype(jnp.int32)
    wins = me * WIN_DEV + jnp.arange(nw, dtype=jnp.int32)
    srcs = jnp.arange(nblocks, dtype=jnp.int32)
    match = sw_got[None, :] == wins[:, None]
    source = jnp.sum(jnp.where(match, srcs[None, :], 0), axis=1)
    sel = jnp.sum(jnp.where(match[:, :, None, None], tail[None], 0.0), axis=1)
    trip = sel[:, :6, :].reshape(nw, 3, 4, K)
    prm_sel = (trip[:, 0] + trip[:, 1]) + trip[:, 2]
    coef = coefficients(
        prm_sel[:, 0],
        prm_sel[:, 1],
        prm_sel[:, 2],
        prm_sel[:, 3],
        sel[:, 6, 0].astype(jnp.int32),
    )

    part_sum = None
    for k in range(NCH):
        g = chunk_gram(source, snapshots, gots[k], coef, k)
        part_sum = g if part_sum is None else part_sum + g
    half = s // 2
    blk_a = part_sum[:, :, :half]
    blk_b = part_sum[:, :, half:s]
    blk_d = part_sum[:, :, s:]
    ii = jnp.arange(half, dtype=jnp.int32)[:, None]
    jj = jnp.arange(half, dtype=jnp.int32)[None, :]
    upper = ii <= jj
    merged = jnp.where(upper[None], blk_a, blk_d)
    diag_d = jnp.sum(jnp.where((ii == jj)[None], blk_d, 0.0), axis=1)
    extra_row = jnp.concatenate([diag_d, jnp.zeros_like(diag_d)], axis=1)[:, None, :]
    packed_g = jnp.concatenate([jnp.concatenate([blk_b, merged], axis=2), extra_row], axis=1)

    nsp = lax.axis_size("space")
    mine = lax.all_to_all(packed_g, "space", split_axis=0, concat_axis=0, tiled=True)
    red = jnp.sum(mine.reshape((nsp, nw // nsp) + mine.shape[1:]), axis=0) / points_all
    spread = jnp.broadcast_to(red[None], (nsp,) + red.shape).reshape((nsp * red.shape[0],) + red.shape[1:])
    total = lax.all_to_all(spread, "space", split_axis=0, concat_axis=0, tiled=True)

    tb = total[:, :half, :half]
    tm = total[:, :half, half:]
    tmt = jnp.swapaxes(tm, 1, 2)
    tdiag = total[:, half, :half]
    ta = jnp.where(upper[None], tm, tmt)
    td = jnp.where((ii > jj)[None], tm, jnp.where((ii < jj)[None], tmt, tdiag[:, None, :]))
    top = jnp.concatenate([ta, tb], axis=2)
    bottom = jnp.concatenate([jnp.swapaxes(tb, 1, 2), td], axis=2)
    return jnp.concatenate([top, bottom], axis=1)


def solution(mesh):
    return jax.shard_map(
        on_device,
        mesh=mesh,
        in_specs=(
            P("win", "space", None),
            P("win", "space", None),
            P("win", None),
            P("win", None),
            P("win", None),
            P("win", None),
            P("win"),
            P("win"),
        ),
        out_specs=P("win", None, None),
        check_vma=False,
    )
```
